32 devices in a mesh: grp: 4 (over x, core), brick: 8 (over z, y).
Axes of the slice: x: 2, y: 2, z: 4, core: 2. Of those that a mesh axis runs over, the one named last changes fastest.
Arguments:
- positions: float32 [3, 262144], P(None, ('grp', 'brick')), may hold values from -6 to 6
- features: float32 [128, 262144], P(None, ('grp', 'brick')), may hold values from -6 to 6
- teacher_nbr: int32 [262144, 12], P(('grp', 'brick')), may hold values from 0 to 10239, as said below
- nbr_count: int32 [262144], P(('grp', 'brick')), may hold values from 3 to 12
- w_rad: float32 [8, 128], replicated, may hold values from -2 to 2
- w_mix: float32 [128, 128], replicated, may hold values from -0.5 to 0.5
- w_out: float32 [128], replicated, may hold values from -0.5 to 0.5
- block_owner: int32 [8192], P(('grp', 'brick')), may hold values from 0 to 31, as said below
- block_start: int32 [8192], P(('grp', 'brick')), may hold values from 0 to 480
- atom_bead: int32 [262144], P(('grp', 'brick')), may hold values from -1 to 31
- bead_pos: float32 [3, 16384], P(None, ('grp', 'brick')), may hold values from -6 to 6
- bead_nbr: int32 [16384, 16], P(('grp', 'brick')), may hold values from 0 to 575, as said below
- bead_weight: float32 [16384], P(('grp', 'brick')), may hold values from 0.5 to 18
- w_first: float32 [8, 128], replicated, may hold values from -2 to 2
- w_second: float32 [128], replicated, may hold values from -0.5 to 0.5
Outputs:
- atom_force: float32 [3, 262144], P(None, ('grp', 'brick'))
- bead_force: float32 [3, 16384], P(None, ('grp', 'brick'))
- student_force: float32 [3, 16384], P(None, ('grp', 'brick'))
- grad_first: float32 [8, 128], replicated
- grad_second: float32 [128], replicated
- loss: float32 [], replicated
The draws below stay inside these ranges and needn't reach their ends.
Inputs may be any that keep to these rules, and one draw needn't show every extreme that they name: `teacher_nbr`: each slot of an atom names an atom within 1024 places of it along the chain of bricks, never itself and never past the chain's ends: a column of 1024 left ghosts, the brick's 8192 atoms and 1024 right ghosts. `block_owner`: every owner is named by exactly 8 of each brick's blocks. `bead_nbr`: each edge of a bead names a bead within 32 places of it in sequence order, never itself and never past the chain's ends: a column of 32 left ghosts, the owner's 512 beads and 32 right ghosts.
All inputs are finite; a program needn't handle non-finite values.
Results may differ from the reference program's by a relative error of at most 0.0003.
Values sent between devices are 32-bit elements; how exact they have to be, the bound alone decides.
No kernel may reach another device: no remote copies, remote signals or barrier semaphores. Data moves between devices by JAX's collectives and lax.ppermute only.
A program may use at most 320 MiB of HBM per device.

```python
import math
import jax
import jax.numpy as jnp
from jax import lax

C = 128
NRAD = 8
H = 128
K = 12
G = 1024
ATOM_BLK = 32
BPB = 32
KB = 16
BW = 32
A_DEV = 8192
BEAD_DEV = 512
TOTAL = 262144
BEADS = 16384


def chain_offsets(key, row_total, slot_total, per_device, reach_width):
    key_mag, key_sign = jax.random.split(key)
    magnitude = jax.random.randint(key_mag, (row_total, slot_total), 1, reach_width + 1)
    direction = jax.random.randint(key_sign, (row_total, slot_total), 0, 2) * 2 - 1
    position = jnp.arange(row_total, dtype=jnp.int32)
    local_pos = position % per_device
    slot_zero = jnp.arange(slot_total, dtype=jnp.int32)[None, :] == 0
    at_low = slot_zero & (local_pos[:, None] == 0)
    at_high = slot_zero & (local_pos[:, None] == per_device - 1)
    magnitude = jnp.where(at_low | at_high, reach_width, magnitude)
    direction = jnp.where(at_low, -1, jnp.where(at_high, 1, direction))
    offset = magnitude * direction
    target = position[:, None] + offset
    outside = (target < 0) | (target >= row_total)
    offset = jnp.where(outside, -offset, offset)
    return (local_pos[:, None] + reach_width + offset).astype(jnp.int32)


def draw_teacher_nbr(key, part):
    return chain_offsets(key, TOTAL, K, A_DEV, G)


def draw_bead_nbr(key, part):
    return chain_offsets(key, BEADS, KB, BEAD_DEV, BW)


def draw_nbr_count(key, part):
    counts = jax.random.randint(key, (TOTAL,), K // 4, K + 1)
    local_pos = jnp.arange(TOTAL, dtype=jnp.int32) % A_DEV
    counts = jnp.where(local_pos == 0, K, jnp.where(local_pos == 1, K // 4, counts))
    return counts.astype(jnp.int32)


def draw_block_owner(key, part):
    devices_all = TOTAL // A_DEV
    blocks_dev = A_DEV // ATOM_BLK
    per_owner = blocks_dev // devices_all
    key_own, key_order = jax.random.split(key)
    owner_keys = jax.random.split(key_own, devices_all)
    order_keys = jax.random.split(key_order, devices_all)
    owner_perm = jax.vmap(lambda one_key: jax.random.permutation(one_key, devices_all))(owner_keys)
    block_perm = jax.vmap(lambda one_key: jax.random.permutation(one_key, blocks_dev))(order_keys)
    chosen = jnp.take_along_axis(owner_perm, block_perm // per_owner, axis=1)
    return chosen.reshape(-1).astype(jnp.int32)


def draw_atom_bead(key, part):
    devices_all = TOTAL // A_DEV
    key_share, key_pick, key_bead = jax.random.split(key, 3)
    protein_share = jax.random.randint(key_share, (devices_all,), 3, 10)
    pick_value = jax.random.randint(key_pick, (TOTAL,), 0, 10)
    device_of = jnp.arange(TOTAL, dtype=jnp.int32) // A_DEV
    bead_rel = jax.random.randint(key_bead, (TOTAL,), 0, BPB)
    return jnp.where(pick_value < protein_share[device_of], bead_rel, -1).astype(jnp.int32)


def draw_bead_weight(key, part):
    ramp = jnp.arange(BEADS, dtype=jnp.float32) / BEADS
    noise = jnp.exp(jax.random.uniform(key, (BEADS,), jnp.float32, math.log(0.5), math.log(2.0)))
    return jnp.exp(math.log(3.0) * ramp) * noise


def plant(entries, own_key, smallest, high):
    dims = entries.shape
    index_at = [jax.random.randint(jax.random.fold_in(own_key, axis), (), 0, dims[axis]) for axis in range(len(dims))]
    entries = entries.at[tuple(index_at)].set(smallest)
    longest = dims.index(max(dims))
    index_at[longest] = (index_at[longest] + 1) % dims[longest]
    return entries.at[tuple(index_at)].set(high)


def level_of(key, dims, cuts, smallest, high):
    def one(dim, parts):
        draws = jax.random.uniform(jax.random.fold_in(jax.random.fold_in(key, 6), dim), (parts,), jnp.float32, smallest / len(cuts), high / len(cuts))
        return jnp.repeat(jnp.exp(draws), dims[dim] // parts).reshape((-1,) + (1,) * (len(dims) - dim - 1))

    factor_of = one(*cuts[0])
    for cut in cuts[1:]:
        factor_of = factor_of * one(*cut)
    return factor_of


def scatter_about(own_key, extent, scale, limit, cuts=(), held_as=jnp.bfloat16):
    result = jax.random.normal(own_key, extent, jnp.float32) * scale
    if len(cuts) > 0:
        result = level_of(own_key, extent, cuts, -0.22, 0.18) * result
    return jnp.clip(result, min=-limit, max=limit).astype(held_as)


def setup_inputs(seed: int = 0) -> dict:
    key_list = jax.random.split(jax.random.key(seed), 16)
    return {
        "positions": scatter_about(key_list[0], (3, TOTAL), 1.0, 6.0, ((1, 32),), jnp.float32),
        "features": scatter_about(key_list[1], (C, TOTAL), 1.0, 6.0, ((1, 32),), jnp.float32),
        "teacher_nbr": draw_teacher_nbr(jax.random.fold_in(key_list[15], 71), 0),
        "nbr_count": draw_nbr_count(jax.random.fold_in(key_list[15], 71), 0),
        "w_rad": scatter_about(key_list[4], (NRAD, C), NRAD ** -0.5, 2.0, (), jnp.float32),
        "w_mix": scatter_about(key_list[5], (C, C), C ** -0.5, 0.5, (), jnp.float32),
        "w_out": scatter_about(key_list[6], (C,), C ** -0.5, 0.5, (), jnp.float32),
        "block_owner": draw_block_owner(jax.random.fold_in(key_list[15], 71), 0),
        "block_start": plant(jax.random.randint(key_list[8], (TOTAL // ATOM_BLK,), 0, BEAD_DEV - BPB + 1), jax.random.fold_in(key_list[8], 1), 0, BEAD_DEV - BPB).astype(jnp.int32),
        "atom_bead": draw_atom_bead(jax.random.fold_in(key_list[15], 71), 0),
        "bead_pos": scatter_about(key_list[10], (3, BEADS), 1.0, 6.0, ((1, 32),), jnp.float32),
        "bead_nbr": draw_bead_nbr(jax.random.fold_in(key_list[15], 71), 0),
        "bead_weight": draw_bead_weight(jax.random.fold_in(key_list[15], 71), 0),
        "w_first": scatter_about(key_list[13], (NRAD, H), NRAD ** -0.5, 2.0, (), jnp.float32),
        "w_second": scatter_about(key_list[14], (H,), H ** -0.5, 0.5, (), jnp.float32),
    }


HIGHEST_PRECISION = lax.Precision.HIGHEST

def decay_rates(rate_count):
    return 0.05 * 1.6 ** jnp.arange(rate_count, dtype=jnp.float32)

def block_energy(own_pos, near_pos, own_feat, near_feat, slot_mask, w_rad, w_mix, w_out):
    offsets = near_pos - own_pos[:, None, :]
    dist_sq = lax.optimization_barrier(jnp.sum(offsets * offsets, axis=0))
    radial_basis = jnp.exp(-decay_rates(w_rad.shape[0])[:, None, None] * dist_sq[None]) * slot_mask[None]
    radial = jnp.einsum('bkn,bc->ckn', radial_basis, w_rad, precision=HIGHEST_PRECISION)
    message = lax.optimization_barrier(jnp.sum(radial * near_feat, axis=1)) / math.sqrt(near_feat.shape[1])
    mixed_feat = jnp.einsum('cn,cd->dn', message, w_mix, precision=HIGHEST_PRECISION) + own_feat
    return jnp.sum(w_out[:, None] * jax.nn.silu(mixed_feat))

def block_grads(own_pos, near_pos, own_feat, near_feat, slot_mask, w_rad, w_mix, w_out):

    def energy(first_arg, second_arg):
        return block_energy(first_arg, second_arg, own_feat, near_feat, slot_mask, w_rad, w_mix, w_out)
    energy_value, pullback = jax.vjp(energy, own_pos, near_pos)
    return pullback(jnp.ones_like(energy_value))

def student_eval(own_pos, near_pos, w_first, w_second):
    offsets = near_pos - own_pos[:, None, :]
    dist_sq = lax.optimization_barrier(jnp.sum(offsets * offsets, axis=0))
    radial_basis = jnp.exp(-decay_rates(w_first.shape[0])[:, None, None] * dist_sq[None])
    hidden = jax.nn.silu(jnp.einsum('bkn,bh->hkn', radial_basis, w_first, precision=HIGHEST_PRECISION))
    strength = jnp.einsum('hkn,h->kn', hidden, w_second, precision=HIGHEST_PRECISION)
    return lax.optimization_barrier(jnp.sum(strength[None] * offsets, axis=1))

def reference(positions, features, teacher_nbr, nbr_count, w_rad, w_mix, w_out, block_owner, block_start, atom_bead, bead_pos, bead_nbr, bead_weight, w_first, w_second):
    atom_total = positions.shape[1]
    ghost_width = G
    padded_pos = jnp.pad(positions, ((0, 0), (ghost_width, ghost_width)))
    padded_feat = jnp.pad(features, ((0, 0), (ghost_width, ghost_width)))
    device_of = (jnp.arange(atom_total, dtype=jnp.int32) // A_DEV).astype(jnp.int32)
    global_nbr = (device_of[:, None] * A_DEV + teacher_nbr).astype(jnp.int32)
    slot_mask = (jnp.arange(K, dtype=jnp.int32)[None, :] < nbr_count[:, None]).astype(jnp.float32)

    def scan_step(grad_sum, block_num):
        first_atom = (block_num * ghost_width).astype(jnp.int32)
        own_pos = lax.dynamic_slice_in_dim(padded_pos, first_atom + ghost_width, ghost_width, 1)
        own_feat = lax.dynamic_slice_in_dim(padded_feat, first_atom + ghost_width, ghost_width, 1)
        neighbours = lax.dynamic_slice_in_dim(global_nbr, first_atom, ghost_width, 0).T
        block_mask = lax.dynamic_slice_in_dim(slot_mask, first_atom, ghost_width, 0).T
        near_pos = padded_pos[:, neighbours]
        near_feat = padded_feat[:, neighbours]
        grad_own, grad_near = block_grads(own_pos, near_pos, own_feat, near_feat, block_mask, w_rad, w_mix, w_out)
        own_cols = (first_atom + ghost_width + jnp.arange(ghost_width, dtype=jnp.int32)).astype(jnp.int32)
        grad_sum = grad_sum.at[:, own_cols].add(grad_own)
        grad_sum = grad_sum.at[:, neighbours].add(grad_near)
        return (grad_sum, None)
    grad_sum, unused = lax.scan(scan_step, jnp.zeros((3, atom_total + 2 * ghost_width), jnp.float32), jnp.arange(atom_total // ghost_width, dtype=jnp.int32))
    atom_force = -grad_sum[:, ghost_width:ghost_width + atom_total]
    bead_total = bead_pos.shape[1]
    block_of = (jnp.arange(atom_total, dtype=jnp.int32) // ATOM_BLK).astype(jnp.int32)
    bead_of = block_owner[block_of] * BEAD_DEV + block_start[block_of] + atom_bead
    bead_of = jnp.where(atom_bead >= 0, bead_of, bead_total).astype(jnp.int32)
    bead_force = jax.ops.segment_sum(atom_force.T, bead_of, num_segments=bead_total + 1)[:bead_total].T
    padded_bead = jnp.pad(bead_pos, ((0, 0), (BW, BW)))
    bead_dev_of = (jnp.arange(bead_total, dtype=jnp.int32) // BEAD_DEV).astype(jnp.int32)
    global_bead_nbr = (bead_dev_of[:, None] * BEAD_DEV + bead_nbr).astype(jnp.int32)

    def bead_step(running, dev_num):
        first_bead = (dev_num * BEAD_DEV).astype(jnp.int32)
        own_pos = lax.dynamic_slice_in_dim(padded_bead, first_bead + BW, BEAD_DEV, 1)
        neighbours = lax.dynamic_slice_in_dim(global_bead_nbr, first_bead, BEAD_DEV, 0).T
        near_pos = padded_bead[:, neighbours]
        target = lax.dynamic_slice_in_dim(bead_force, first_bead, BEAD_DEV, 1)
        weights = lax.dynamic_slice_in_dim(bead_weight, first_bead, BEAD_DEV, 0)

        def block_loss(first_w, second_w):
            predicted = student_eval(own_pos, near_pos, first_w, second_w)
            residual = predicted - target
            return (jnp.sum(weights * lax.optimization_barrier(jnp.sum(residual * residual, axis=0))) / (3.0 * bead_total), predicted)
        loss_part, pullback, predicted = jax.vjp(block_loss, w_first, w_second, has_aux=True)
        grad_one, grad_two = pullback(jnp.ones_like(loss_part))
        return ((running[0] + grad_one, running[1] + grad_two, running[2] + loss_part), predicted)
    start_sums = (jnp.zeros(w_first.shape, jnp.float32), jnp.zeros(w_second.shape, jnp.float32), jnp.zeros((), jnp.float32))
    sums, predicted = lax.scan(bead_step, start_sums, jnp.arange(bead_total // BEAD_DEV, dtype=jnp.int32))
    student_force = jnp.transpose(predicted, (1, 0, 2)).reshape(3, bead_total)
    return (atom_force, bead_force, student_force, sums[0], sums[1], sums[2])
```

```python
import math

import jax
import jax.numpy as jnp
from jax import lax
from jax.experimental import pallas as pl
from jax.experimental.pallas import tpu as pltpu
from jax.sharding import PartitionSpec as P

G = 1024
BW = 32
L = 128
WIN = 24
AXES = ("grp", "brick")
NN = (((1,), (0,)), ((), ()))
NT = (((1,), (1,)), ((), ()))
TN = (((0,), (0,)), ((), ()))


def mm(a, b, dims=NN):
    return lax.dot_general(a, b, dims, preferred_element_type=jnp.float32)


def hi_lo(v):
    hi = v.astype(jnp.bfloat16)
    return hi, (v - hi.astype(jnp.float32)).astype(jnp.bfloat16)


def split(w):
    hi = lax.reduce_precision(w, 8, 7)
    return hi.astype(jnp.bfloat16), (w - hi).astype(jnp.bfloat16)


def all_rows(v):
    v = v + pltpu.roll(v, 4, 0)
    v = v + pltpu.roll(v, 2, 0)
    return v + pltpu.roll(v, 1, 0)


def expand(e):
    hi = e.astype(jnp.bfloat16).astype(jnp.float32)
    lo = e - hi
    return jnp.concatenate([hi, lo, hi, lo], axis=0).astype(jnp.bfloat16)


def decay_rates(rate_count):
    rates = 0.05 * 1.6 ** jnp.arange(rate_count, dtype=jnp.float32)
    return jnp.broadcast_to(rates[:, None], (rate_count, L))


def shifted(array, by):
    peers = lax.axis_size(AXES)
    pairs = [(i, i + by) for i in range(peers) if 0 <= i + by < peers]
    return lax.ppermute(array, AXES, pairs)


def teacher_kernel(
    idx_hbm, tab, pos, nbr, cnt, rate, w4, ww, wm, wml, wt, wtl, wout, out,
    idx_s, hbuf, ebuf, dbuf, rbuf, lhot, abuf, sem, *, slots, nblk, group,
):
    i = pl.program_id(0)
    reach = G // L
    base = i + 2 * reach * (i // group)

    @pl.when(i == 0)
    def _():
        pltpu.make_async_copy(idx_hbm.at[0], idx_s, sem).start()
        out[...] = jnp.zeros(out.shape, jnp.float32)

    pltpu.make_async_copy(idx_hbm.at[i], idx_s, sem).wait()
    for s in range(slots):
        for j in range(L):
            hbuf[s, j : j + 1, :] = tab[pl.ds(idx_s[s * L + j], 1), :]

    @pl.when(i + 1 < nblk)
    def _():
        pltpu.make_async_copy(idx_hbm.at[i + 1], idx_s, sem).start()

    iota8 = lax.broadcasted_iota(jnp.int32, (8, L), 0)
    iota24 = lax.broadcasted_iota(jnp.int32, (WIN, L), 0)
    iota128 = lax.broadcasted_iota(jnp.int32, (L, L), 0)
    count = jnp.broadcast_to(cnt[...], (8, L))
    rates = rate[...]
    xs = [pos[c, pl.ds(base, WIN), :] for c in range(3)]
    own = [jnp.broadcast_to(pos[c, pl.ds(base + reach, 1), :], (8, L)) for c in range(3)]
    msg = jnp.zeros((L, L), jnp.float32)
    for s in range(slots):
        n = jnp.broadcast_to(nbr[s : s + 1, :] - base * L, (WIN, L))
        row = n >> 7
        lane = n & (L - 1)
        here = row == iota24
        hot = iota128 == jnp.broadcast_to(lane[0:1], (L, L))
        lhot[:, s * L : (s + 1) * L] = hot.astype(jnp.bfloat16)
        rbuf[s] = row[0:8]
        q = jnp.zeros((8, L), jnp.float32)
        for c in range(3):
            g = jnp.where(here, jnp.take_along_axis(xs[c], lane, axis=1), 0.0)
            d = all_rows(g[0:8] + g[8:16] + g[16:24]) - own[c]
            dbuf[s, c] = d
            q = q + d * d
        e = jnp.where(count > s, jnp.exp(-rates * q), 0.0)
        ebuf[s] = e
        msg = msg + mm(expand(e), w4[...], TN) * hbuf[s]
    mhi, mlo = hi_lo(msg)
    pre = mm(jnp.concatenate([mhi, mlo], axis=1), wm[...]) + mm(mhi, wml[...])
    pre = pre + tab[pl.ds(pl.multiple_of((base + reach) * L, L), L), :]
    sig = 1.0 / (1.0 + jnp.exp(-pre))
    g = wout[...] * (sig * (1.0 + pre * (1.0 - sig)))
    ghi, glo = hi_lo(g)
    mbar = mm(jnp.concatenate([ghi, glo], axis=1), wt[...]) + mm(ghi, wtl[...])
    total = [jnp.zeros((8, L), jnp.float32)] * 3
    for s in range(slots):
        zhi, zlo = hi_lo(mbar * hbuf[s])
        t = mm(ww[...], jnp.concatenate([zhi, zlo], axis=1), NT)
        f = all_rows((t[0:8] + t[8:16]) * ebuf[s] * (-2.0 * rates))
        row = rbuf[s]
        parts = []
        for c in range(3):
            fc = f * dbuf[s, c]
            total[c] = total[c] + fc
            for k in range(WIN // 8):
                parts.append(jnp.where(row == iota8 + 8 * k, fc, 0.0))
        ahi, alo = hi_lo(jnp.concatenate(parts, axis=0))
        abuf[:, s * L : (s + 1) * L] = jnp.concatenate([ahi, alo], axis=0)
    sc = mm(abuf[...], lhot[...], NT)
    for c in range(3):
        upd = sc[WIN * c : WIN * (c + 1)] + sc[WIN * (3 + c) : WIN * (4 + c)]
        upd = upd - jnp.where(iota24 == reach, jnp.broadcast_to(total[c][0:1], (WIN, L)), 0.0)
        out[c, pl.ds(base, WIN), :] += upd


def teacher_weights(w_rad, w_mix, w_out, slots):
    rhi, rlo = split(w_rad)
    w4 = jnp.concatenate([rhi, rhi, rlo, rlo], axis=0)
    ww = jnp.concatenate(
        [jnp.concatenate([rhi, rhi], 1), jnp.concatenate([rlo, rlo], 1)], 0
    )
    scaled = w_mix / math.sqrt(slots)
    xhi, xlo = split(scaled)
    thi, tlo = split(scaled.T)
    wm = jnp.concatenate([xhi, xhi], 0)
    wt = jnp.concatenate([thi, thi], 0)
    return decay_rates(w_rad.shape[0]), w4, ww, wm, xlo, wt, tlo, w_out[None, :]


def teacher(tab, pos, idx, nbr, cnt, weights, group):
    rows = tab.shape[0]
    nblk, per = idx.shape
    slots = per // L
    padded = rows // L + 8
    pos3 = jnp.pad(pos, ((0, 0), (0, padded - pos.shape[1]), (0, 0)))

    def full(array):
        return pl.BlockSpec(
            array.shape, lambda i: (0,) * array.ndim, pipeline_mode=pl.Buffered(1)
        )

    grad = pl.pallas_call(
        lambda *refs: teacher_kernel(*refs, slots=slots, nblk=nblk, group=group),
        grid=(nblk,),
        in_specs=[
            pl.BlockSpec(memory_space=pl.ANY),
            full(tab),
            full(pos3),
            pl.BlockSpec((slots, L), lambda i: (0, i)),
            pl.BlockSpec((1, L), lambda i: (0, i)),
        ]
        + [full(w) for w in weights],
        out_specs=pl.BlockSpec((3, padded, L), lambda i: (0, 0, 0)),
        out_shape=jax.ShapeDtypeStruct((3, padded, L), jnp.float32),
        scratch_shapes=[
            pltpu.SMEM((per,), jnp.int32),
            pltpu.VMEM((slots, L, L), jnp.float32),
            pltpu.VMEM((slots, 8, L), jnp.float32),
            pltpu.VMEM((slots, 3, 8, L), jnp.float32),
            pltpu.VMEM((slots, 8, L), jnp.int32),
            pltpu.VMEM((L, per), jnp.bfloat16),
            pltpu.VMEM((6 * WIN, per), jnp.bfloat16),
            pltpu.SemaphoreType.DMA,
        ],
        name="teacher",
    )(idx, tab, pos3, nbr, cnt, *weights)
    return grad[:, : rows // L]


def blocks_of(nbr):
    slots, atoms = nbr.shape
    return nbr.reshape(slots, atoms // L, L).transpose(1, 0, 2).reshape(-1, slots * L)


def map_kernel(force, where, col, out, abuf):
    @pl.when(pl.program_id(0) == 0)
    def _():
        out[...] = jnp.zeros(out.shape, jnp.float32)

    rows = out.shape[0] // 6
    span = force.shape[1]
    target = jnp.broadcast_to(where[...], (rows, span))
    here = target == lax.broadcasted_iota(jnp.int32, (rows, span), 0)
    for c in range(3):
        value = jnp.where(here, jnp.broadcast_to(force[c : c + 1, :], (rows, span)), 0.0)
        hi, lo = hi_lo(value)
        abuf[rows * c : rows * (c + 1), :] = hi
        abuf[rows * (3 + c) : rows * (4 + c), :] = lo
    lane = jnp.broadcast_to(col[...], (L, span))
    hot = (lane == lax.broadcasted_iota(jnp.int32, (L, span), 0)).astype(jnp.bfloat16)
    out[...] += mm(abuf[...], hot, NT)


def map_forces(force, where, col, rows):
    span = 512
    steps = force.shape[1] // span
    parts = pl.pallas_call(
        map_kernel,
        grid=(steps,),
        in_specs=[
            pl.BlockSpec((3, span), lambda i: (0, i)),
            pl.BlockSpec((1, span), lambda i: (0, i)),
            pl.BlockSpec((1, span), lambda i: (0, i)),
        ],
        out_specs=pl.BlockSpec((6 * rows, L), lambda i: (0, 0)),
        out_shape=jax.ShapeDtypeStruct((6 * rows, L), jnp.float32),
        scratch_shapes=[pltpu.VMEM((6 * rows, span), jnp.bfloat16)],
        name="mapping",
    )(force, where, col)
    return parts.reshape(2, 3, rows, L).sum(0)


def student_kernel(
    pos, nbr, bead, weight, rate, w4t, w2, pred, grads, gbuf, dbuf, hid, slope, *, slots, scale
):
    i = pl.program_id(0)

    @pl.when(i == 0)
    def _():
        grads[...] = jnp.zeros(grads.shape, jnp.float32)

    rates = rate[...]
    wide = jnp.concatenate(
        [pos[c, pl.ds(i, 2), :] for c in range(3)] + [jnp.zeros((2, L), jnp.float32)], axis=0
    )
    low = [jnp.broadcast_to(wide[2 * c : 2 * c + 1], (8, L)) for c in range(3)]
    high = [jnp.broadcast_to(wide[2 * c + 1 : 2 * c + 2], (8, L)) for c in range(3)]
    own = [
        jnp.concatenate([low[c][:, BW:], high[c][:, :BW]], axis=1) for c in range(3)
    ]
    outcol = w2[...]
    force = [jnp.zeros((8, L), jnp.float32)] * 3
    for s in range(slots):
        n = jnp.broadcast_to(nbr[s : s + 1, :] - i * L, (8, L))
        first = n < L
        near = jnp.take_along_axis(wide, n & (L - 1), axis=1)
        q = jnp.zeros((8, L), jnp.float32)
        ds = []
        for c in range(3):
            x = jnp.where(
                first,
                jnp.broadcast_to(near[2 * c : 2 * c + 1], (8, L)),
                jnp.broadcast_to(near[2 * c + 1 : 2 * c + 2], (8, L)),
            )
            d = x - own[c]
            dbuf[s, c] = d
            ds.append(d)
            q = q + d * d
        g = jnp.exp(-rates * q)
        gbuf[s] = g
        z = mm(w4t[...], expand(g))
        sig = 1.0 / (1.0 + jnp.exp(-z))
        h = z * sig
        hid[s] = h
        slope[s] = outcol * (sig * (1.0 + z * (1.0 - sig)))
        weighted = outcol * h
        strength = weighted[0:8]
        for k in range(1, L // 8):
            strength = strength + weighted[8 * k : 8 * k + 8]
        strength = all_rows(strength)
        for c in range(3):
            force[c] = force[c] + strength * ds[c]
    wgt = jnp.broadcast_to(weight[...], (8, L))
    loss = jnp.zeros((8, L), jnp.float32)
    coef = []
    for c in range(3):
        pred[c : c + 1, :] = force[c][0:1]
        resid = force[c] - jnp.broadcast_to(bead[c : c + 1, :], (8, L))
        loss = loss + wgt * resid * resid
        coef.append((2.0 * scale) * wgt * resid)
    acc1 = jnp.zeros((16, L), jnp.float32)
    acc2 = jnp.zeros((16, L), jnp.float32)
    for s in range(slots):
        edge = coef[0] * dbuf[s, 0] + coef[1] * dbuf[s, 1] + coef[2] * dbuf[s, 2]
        hi, lo = hi_lo(jnp.concatenate([gbuf[s] * edge, edge], axis=0))
        shi, slo = hi_lo(slope[s])
        hhi, hlo = hi_lo(hid[s])
        left1 = jnp.concatenate([hi[0:8], lo[0:8]], axis=0)
        left2 = jnp.concatenate([hi[8:16], lo[8:16]], axis=0)
        acc1 = acc1 + mm(left1, shi, NT) + mm(left1, slo, NT)
        acc2 = acc2 + mm(left2, hhi, NT) + mm(left2, hlo, NT)
    grads[0:8, :] += acc1[0:8] + acc1[8:16]
    iota8 = lax.broadcasted_iota(jnp.int32, (8, L), 0)
    second = jnp.where(iota8 == 0, acc2[0:8] + acc2[8:16], 0.0)
    grads[8:16, :] += second + jnp.where(iota8 == 1, scale * loss, 0.0)


def student(bead_ext, nbr, bead, weight, w_first, w_second, bead_total):
    slots, beads = nbr.shape
    steps = beads // L
    cols = (steps + 1) * L
    pos = jnp.pad(bead_ext, ((0, 0), (0, cols - bead_ext.shape[1]))).reshape(3, steps + 1, L)
    hi, lo = split(w_first)
    w4t = jnp.concatenate([hi, hi, lo, lo], axis=0).T
    w2 = jnp.broadcast_to(w_second[:, None], (w_second.shape[0], L))
    return pl.pallas_call(
        lambda *refs: student_kernel(*refs, slots=slots, scale=1.0 / (3.0 * bead_total)),
        grid=(steps,),
        in_specs=[
            pl.BlockSpec(pos.shape, lambda i: (0, 0, 0)),
            pl.BlockSpec((slots, L), lambda i: (0, i)),
            pl.BlockSpec((3, L), lambda i: (0, i)),
            pl.BlockSpec((1, L), lambda i: (0, i)),
            pl.BlockSpec((8, L), lambda i: (0, 0)),
            pl.BlockSpec(w4t.shape, lambda i: (0, 0)),
            pl.BlockSpec(w2.shape, lambda i: (0, 0)),
        ],
        out_specs=[
            pl.BlockSpec((3, L), lambda i: (0, i)),
            pl.BlockSpec((16, L), lambda i: (0, 0)),
        ],
        out_shape=[
            jax.ShapeDtypeStruct((3, beads), jnp.float32),
            jax.ShapeDtypeStruct((16, L), jnp.float32),
        ],
        scratch_shapes=[
            pltpu.VMEM((slots, 8, L), jnp.float32),
            pltpu.VMEM((slots, 3, 8, L), jnp.float32),
            pltpu.VMEM((slots, L, L), jnp.float32),
            pltpu.VMEM((slots, L, L), jnp.float32),
        ],
        name="student",
    )(pos, nbr, bead, weight, decay_rates(w_first.shape[0]), w4t, w2)


def local(
    positions,
    features,
    teacher_nbr,
    nbr_count,
    w_rad,
    w_mix,
    w_out,
    block_owner,
    block_start,
    atom_bead,
    bead_pos,
    bead_nbr,
    bead_weight,
    w_first,
    w_second,
):
    atoms = positions.shape[1]
    devices = lax.axis_size(AXES)
    slots = teacher_nbr.shape[1]
    gr = G // L
    rows = atoms // L
    weights = teacher_weights(w_rad, w_mix, w_out, slots)
    table = features.T
    pos_rows = positions.reshape(3, rows, L)

    def packed(feat, pos):
        return jnp.concatenate([feat, pos.reshape(3 * gr, L)], axis=0)

    from_left = shifted(packed(table[atoms - G :], pos_rows[:, rows - gr :]), 1)
    from_right = shifted(packed(table[:G], pos_rows[:, :gr]), -1)
    bead_left = shifted(bead_pos[:, bead_pos.shape[1] - BW :], 1)
    bead_right = shifted(bead_pos[:, :BW], -1)

    nbr = teacher_nbr.T
    count = nbr_count[None, :]
    mid = nbr[:, G : atoms - G] - G
    inner = teacher(
        table, pos_rows, blocks_of(mid), mid, count[:, G : atoms - G], weights, rows
    )

    left_pos = from_left[G:].reshape(3, gr, L)
    right_pos = from_right[G:].reshape(3, gr, L)
    edge_table = jnp.concatenate(
        [from_left[:G], table[: 2 * G], table[atoms - 2 * G :], from_right[:G]], axis=0
    )
    edge_pos = jnp.concatenate(
        [left_pos, pos_rows[:, : 2 * gr], pos_rows[:, rows - 2 * gr :], right_pos], axis=1
    )
    edge_nbr = jnp.concatenate([nbr[:, :G], nbr[:, atoms - G :] - (atoms - 4 * G)], axis=1)
    edge_count = jnp.concatenate([count[:, :G], count[:, atoms - G :]], axis=1)
    outer = teacher(edge_table, edge_pos, blocks_of(edge_nbr), edge_nbr, edge_count, weights, gr)

    from_above = shifted(outer[:, :gr], -1)
    from_below = shifted(outer[:, 5 * gr :], 1)
    total = inner
    total = total.at[:, : 2 * gr].add(outer[:, gr : 3 * gr])
    total = total.at[:, rows - 2 * gr :].add(outer[:, 3 * gr : 5 * gr])
    total = total.at[:, :gr].add(from_below)
    total = total.at[:, rows - gr :].add(from_above)
    atom_force = -total.reshape(3, atoms)

    bead_dev = bead_pos.shape[1]
    per = bead_dev // L
    block = atoms // block_owner.shape[0]
    owner = jnp.repeat(block_owner, block)
    start = jnp.repeat(block_start, block)
    bead = start + atom_bead
    where = jnp.where(atom_bead >= 0, owner * per + (bead >> 7), -1)[None, :]
    col = (bead & (L - 1))[None, :]
    parts = map_forces(atom_force, where, col, devices * per)
    parts = parts.reshape(3, devices, per, L).transpose(1, 0, 2, 3)
    arrived = lax.all_to_all(parts, AXES, 0, 0, tiled=True)
    bead_force = arrived.sum(0).reshape(3, bead_dev)

    bead_ext = jnp.concatenate([bead_left, bead_pos, bead_right], axis=1)
    predicted, grads = student(
        bead_ext, bead_nbr.T, bead_force, bead_weight[None, :], w_first, w_second,
        bead_dev * devices,
    )
    grads = lax.psum(grads, AXES)
    nrad = w_first.shape[0]
    return (
        atom_force,
        bead_force,
        predicted,
        grads[:nrad],
        grads[nrad],
        jnp.sum(grads[nrad + 1]),
    )


def solution(mesh):
    atoms_last = P(None, AXES)
    atoms_first = P(AXES, None)
    flat = P(AXES)
    placed = (
        atoms_last, atoms_last, atoms_first, flat, P(), P(), P(), flat, flat, flat,
        atoms_last, atoms_first, flat, P(), P(),
    )
    return jax.shard_map(
        local,
        mesh=mesh,
        in_specs=placed,
        out_specs=(atoms_last, atoms_last, atoms_last, P(), P(), P()),
        check_vma=False,
    )
```
